256 devices in a mesh: dp: 32 (over y, z_hi, core), expert: 8 (over x, z_lo).
Axes of the slice: x: 4, y: 4, z: 8 (z_hi: 4, z_lo: 2; z = z_hi * 2 + z_lo), core: 2. Of those that a mesh axis runs over, the one named last changes fastest.
Arguments:
- tokens: bfloat16 [4096, 3072], P('dp', 'expert'), may hold values from -6 to 6
- out_grad: bfloat16 [4096, 3072], P('dp', 'expert'), may hold values from -6 to 6
- expert_ids: int32 [4096, 2], P('dp'), may hold values from 0 to 7, all different within a row; in each aligned block of 128 rows (0 to 127, 128 to 255, ...) at most 33 rows name the same one
- route_weights: float32 [4096, 2], P('dp'), may hold values from 0.2 to 1
- w_gate: bfloat16 [8, 3072, 8192], P('expert', None, 'dp'), may hold values from -0.109375 to 0.109375
- w_up: bfloat16 [8, 3072, 8192], P('expert', None, 'dp'), may hold values from -0.109375 to 0.109375
- w_down: bfloat16 [8, 8192, 3072], P('expert', 'dp'), may hold values from -0.0625 to 0.0625
Outputs:
- combined: bfloat16 [4096, 3072], P('dp', 'expert')
- d_gate: bfloat16 [8, 3072, 8192], P('expert', None, 'dp')
- d_up: bfloat16 [8, 3072, 8192], P('expert', None, 'dp')
- d_down: bfloat16 [8, 8192, 3072], P('expert', 'dp')
- d_route: float32 [4096, 2], P('dp')
The draws below stay inside these ranges and needn't reach their ends.
Inputs may be any that keep to these rules, and one draw needn't show every extreme that they name: `expert_ids`: each token names 2 different experts; among the 128 tokens of one index of dp no expert is named more than 33 times, a bound that some block reaches.
All inputs are finite; a program needn't handle non-finite values.
Results may differ from the reference program's by a relative error of at most 0.02.
Values may be sent and summed in bfloat16 or wider, within the bound.
A program may use at most 128 MiB of HBM per device.

```python
import math
import jax
import jax.numpy as jnp
import numpy as np
from jax import lax

D = 3072
FF = 8192
TOP = 2
TOK = 128
EXPERTS = 8
CAP = 33
TOKENS = 4096
N_DP = 32


def level_of(own_key, shape, cuts, low, high):
    factor_of = 1.0
    for position, shards_of in cuts:
        draws = jax.random.uniform(jax.random.fold_in(jax.random.fold_in(own_key, 6), position), (shards_of,), jnp.float32, low / len(cuts), high / len(cuts))
        factor_of = factor_of * jnp.repeat(jnp.exp(draws), shape[position] // shards_of).reshape((-1,) + (1,) * (len(shape) - 1 - position))
    return factor_of


def deal_out(own_key, own, number, rows, number_of, top, most, skew):
    sequence = jax.random.permutation(own_key, number_of)
    packed, ordinary = load_shares(number_of, rows * top, most, skew, True), load_shares(number_of, rows * top, most, skew, False)
    places = jnp.arange(number_of)

    def named(sizes, offset_by):
        used = int((sizes > 0).sum())
        fixed = max(1, used // 4)
        moved = fixed + (places - fixed + offset_by * (used - fixed)) % max(1, number_of - fixed)
        return jnp.zeros((number_of,), jnp.int32).at[sequence[jnp.where(places < fixed, places, moved)]].set(jnp.asarray(sizes, jnp.int32))

    sizes = jnp.where(number % 4 == 0, named(packed, number // 4), named(ordinary, number - number // 4 - 1))
    mixed = jax.random.permutation(jax.random.fold_in(own, 3), number_of)
    source_of, taker = mixed[0:number_of // 2 * 2:2], mixed[1:number_of // 2 * 2:2]
    slack = jnp.minimum(sizes[source_of] - 1, most - sizes[taker]) // 2
    slack = jnp.where((source_of == sequence[0]) | (taker == sequence[0]) | (sizes[taker] == 0), 0, jnp.maximum(slack, 0))
    moved = jax.random.randint(jax.random.fold_in(own, 4), (number_of // 2,), 0, 1 << 20) % (slack + 1)
    sizes = sizes.at[source_of].add(-moved).at[taker].add(moved)
    items = jnp.searchsorted(jnp.cumsum(sizes), jnp.arange(rows * top), side="right").astype(jnp.int32)
    listing = items.reshape(top, rows).T
    listing = listing[jax.random.permutation(jax.random.fold_in(own, 1), rows)]
    offset_by = jax.random.randint(jax.random.fold_in(own, 2), (rows, 1), 0, top)
    return jnp.take_along_axis(listing, (jnp.arange(top)[None, :] + offset_by) % top, axis=1)


def load_shares(count, total, limit, lean, full):
    weights = [(1 << 20) // math.isqrt(rank ** lean) + 1 for rank in range(1, count + 1)]
    largest = limit if full else min(limit, max(-(-total // count), total * weights[0] // sum(weights)))
    least = 1 if total - largest >= count - 1 else 0
    given, surplus = [largest] + [least] * (count - 1), total - largest - least * (count - 1)
    while surplus > 0:
        candidates = [i for i in range(1, count) if given[i] < largest] or [i for i in range(1, count) if given[i] < limit]
        pool, remaining = sum([weights[i] for i in candidates]), surplus
        for i in candidates:
            extra = min(limit - given[i], max(1, remaining * weights[i] // pool), surplus)
            given[i] = given[i] + extra
            surplus = surplus - extra
    return np.array(given)


def normal_values(own_key, dims, scale, bound, split=(), held_as=jnp.bfloat16):
    loudness = level_of(own_key, dims, split, -0.22, 0.18) if split else 1.0
    entries = jax.random.normal(own_key, dims, jnp.float32) * scale * loudness
    return jnp.minimum(jnp.maximum(entries, -bound), bound).astype(held_as)


def setup_inputs(seed: int = 0) -> dict:
    key_of = jax.random.split(jax.random.key(seed), 8)
    tokens = normal_values(key_of[0], (TOKENS, D), 1.0, 6.0, ((0, 32), (1, 8)))
    out_grad = normal_values(key_of[1], (TOKENS, D), 1.0, 6.0, ((0, 32), (1, 8)))
    expert_ids_keys = jax.random.split(jax.random.fold_in(key_of[2], 1), TOKENS // TOK)
    expert_ids_turns = jax.random.permutation(jax.random.fold_in(key_of[2], 3), TOKENS // TOK)
    expert_ids = jax.vmap(lambda own, number: deal_out(jax.random.fold_in(key_of[2], 2), own, number, TOK, EXPERTS, TOP, CAP, 2))(expert_ids_keys, expert_ids_turns).reshape((TOKENS, TOP))
    route_weights = jnp.clip(0.2 + 0.8 * jax.random.uniform(key_of[3], (TOKENS, TOP), jnp.float32) ** level_of(key_of[3], (TOKENS, TOP), ((0, 32),), -0.2, 0.2), 0.2, 1.0)
    w_gate = normal_values(key_of[4], (EXPERTS, D, FF), D ** -0.5, 0.109375, ((0, 8), (2, 32)))
    w_up = normal_values(key_of[5], (EXPERTS, D, FF), D ** -0.5, 0.109375, ((0, 8), (2, 32)))
    w_down = normal_values(key_of[6], (EXPERTS, FF, D), FF ** -0.5, 0.0625, ((0, 8), (1, 32)))
    return dict(tokens=tokens, out_grad=out_grad, expert_ids=expert_ids, route_weights=route_weights, w_gate=w_gate, w_up=w_up, w_down=w_down)


highest = lax.Precision.HIGHEST


def slot_table(routed, experts):
    flattened = routed.reshape(-1)
    onehot = (flattened[:, None] == jnp.arange(experts, dtype=jnp.int32)[None, :]).astype(jnp.int32)
    before = jnp.cumsum(onehot, axis=0) - onehot
    return jnp.sum(before * onehot, axis=1).reshape(routed.shape).astype(jnp.int32)


def pick_tables(routed, experts, capacity):
    places = slot_table(routed, experts)
    target = (routed * capacity + places).astype(jnp.int32)
    row_ids = jnp.arange(experts * capacity, dtype=jnp.int32)[:, None]
    return [(row_ids == target[None, :, which]).astype(jnp.float32) for which in range(routed.shape[1])]


def slab_sum(left_slabs, right_slabs):
    def add_slab(total, pair):
        term = jnp.dot(pair[0], pair[1], preferred_element_type=jnp.float32).astype(jnp.bfloat16)
        term = lax.optimization_barrier(term)
        return total + term.astype(jnp.float32), None
    start = jnp.zeros((left_slabs.shape[1], right_slabs.shape[2]), jnp.float32)
    return lax.scan(add_slab, start, (left_slabs, right_slabs))[0]


def reference(tokens, out_grad, expert_ids, route_weights, w_gate, w_up, w_down):
    slab_size = FF // N_DP
    routed = expert_ids.reshape(N_DP, TOK, TOP)
    shares = route_weights.reshape(N_DP, TOK, TOP)
    inputs = tokens.reshape(N_DP, TOK, D)
    grad_rows = out_grad.reshape(N_DP, TOK, D)

    def dispatch_block(block_in):
        picks = pick_tables(block_in[0], EXPERTS, CAP)
        dispatch = sum(picks)
        weighted = sum(picks[which] * block_in[1][None, :, which] for which in range(TOP))
        sent_in = jnp.dot(dispatch, block_in[2].astype(jnp.float32), precision=highest).astype(jnp.bfloat16)
        sent_gr = jnp.dot(weighted, block_in[3].astype(jnp.float32), precision=highest).astype(jnp.bfloat16)
        return sent_in, sent_gr

    sent_in, sent_gr = lax.map(dispatch_block, (routed, shares, inputs, grad_rows))

    def by_expert(array):
        return array.reshape(N_DP, EXPERTS, CAP, D).transpose(1, 0, 2, 3).reshape(EXPERTS, N_DP * CAP, D)

    def expert_block(block_in):
        x_rows, g_rows, gate_w, up_w, down_w = block_in
        gate_pre = jnp.dot(x_rows, gate_w, preferred_element_type=jnp.float32)
        up_pre = jnp.dot(x_rows, up_w, preferred_element_type=jnp.float32)
        sigmoid_gate = jax.nn.sigmoid(gate_pre)
        hidden = (gate_pre * sigmoid_gate * up_pre).astype(jnp.bfloat16)
        count = x_rows.shape[0]
        hidden_slabs = hidden.reshape(count, N_DP, slab_size).transpose(1, 0, 2)
        down_slabs = down_w.reshape(N_DP, slab_size, D)
        expert_out = slab_sum(hidden_slabs, down_slabs).astype(jnp.bfloat16)
        d_hidden = jnp.dot(g_rows, down_w.T, preferred_element_type=jnp.float32)
        d_down = jnp.dot(hidden.T, g_rows, preferred_element_type=jnp.float32).astype(jnp.bfloat16)
        d_gate_act = (d_hidden * up_pre * sigmoid_gate * (1.0 + gate_pre * (1.0 - sigmoid_gate))).astype(jnp.bfloat16)
        d_up_act = (d_hidden * gate_pre * sigmoid_gate).astype(jnp.bfloat16)
        d_gate = jnp.dot(x_rows.T, d_gate_act, preferred_element_type=jnp.float32).astype(jnp.bfloat16)
        d_up = jnp.dot(x_rows.T, d_up_act, preferred_element_type=jnp.float32).astype(jnp.bfloat16)
        return expert_out, d_gate, d_up, d_down

    expert_out, d_gate, d_up, d_down = lax.map(
        expert_block, (by_expert(sent_in), by_expert(sent_gr), w_gate, w_up, w_down))

    def to_tokens(array):
        return array.reshape(EXPERTS, N_DP, CAP, D).transpose(1, 0, 2, 3).reshape(N_DP, EXPERTS * CAP, D)

    def combine_block(block_in):
        routed_b, shares_b, grads_b, out_b = block_in
        picks = pick_tables(routed_b, EXPERTS, CAP)
        weighted = sum(picks[which] * shares_b[None, :, which] for which in range(TOP))
        flat_out = out_b.astype(jnp.float32)
        combined = jnp.dot(weighted.T, flat_out, precision=highest).astype(jnp.bfloat16)
        grads32 = grads_b.astype(jnp.float32)
        route_dots = jnp.stack([jnp.sum(grads32 * jnp.dot(picks[which].T, flat_out, precision=highest), axis=1)
                                for which in range(TOP)], axis=1)
        return combined, route_dots

    combined, d_route = lax.map(combine_block, (routed, shares, grad_rows, to_tokens(expert_out)))
    return (combined.reshape(TOKENS, D), d_gate, d_up, d_down, d_route.reshape(TOKENS, TOP))
```

```python
import jax
import jax.numpy as jnp
from jax import lax
from jax.sharding import Mesh
from jax.sharding import PartitionSpec as P

highest = lax.Precision.HIGHEST
DP = ("dpo", "core")


def slot_table(routed, experts):
    flattened = routed.reshape(-1)
    onehot = (flattened[:, None] == jnp.arange(experts, dtype=jnp.int32)[None, :]).astype(jnp.int32)
    before = jnp.cumsum(onehot, axis=0) - onehot
    return jnp.sum(before * onehot, axis=1).reshape(routed.shape)


def pick_tables(routed, experts, capacity):
    places = slot_table(routed, experts)
    target = routed * capacity + places
    row_ids = jnp.arange(experts * capacity, dtype=jnp.int32)[:, None]
    return [
        (row_ids == target[None, :, which]).astype(jnp.float32) for which in range(routed.shape[1])
    ]


def local(tokens, out_grad, expert_ids, route_weights, w_gate, w_up, w_down):
    experts = lax.axis_size("expert")
    n_core = lax.axis_size("core")
    tok_rows, feat = tokens.shape
    top_count = expert_ids.shape[1]
    capacity = min(tok_rows, tok_rows * top_count * 33 // (32 * experts))
    picks = pick_tables(expert_ids, experts, capacity)
    dispatch = sum(picks)
    weighted = sum((picks[which] * route_weights[None, :, which] for which in range(top_count)))
    sent_tokens = jnp.dot(dispatch.astype(jnp.bfloat16), tokens, preferred_element_type=jnp.float32)
    sent_tokens = sent_tokens.astype(jnp.bfloat16).reshape(experts, 1, capacity, feat)
    sent_grads = jnp.dot(weighted, out_grad.astype(jnp.float32), precision=highest)
    sent_grads = sent_grads.astype(jnp.bfloat16).reshape(experts, 1, capacity, feat)
    sent = jnp.concatenate([sent_tokens, sent_grads], axis=1)
    recv = lax.all_to_all(sent, "expert", split_axis=0, concat_axis=3, tiled=True)
    half = lax.all_gather(recv, "dpo", axis=0, tiled=True)
    full = lax.all_gather(half, "core", axis=0, tiled=True)
    n_rows = full.shape[0] * capacity
    d_all = full.shape[3]
    gathered = full[:, 0].reshape(n_rows, d_all)
    grads_in = full[:, 1].reshape(n_rows, d_all)
    gate_slab = w_gate[0]
    up_slab = w_up[0]
    down_slab = w_down[0]

    gate_pre = jnp.dot(gathered, gate_slab, preferred_element_type=jnp.float32)
    up_pre = jnp.dot(gathered, up_slab, preferred_element_type=jnp.float32)
    sigmoid_gate = jax.nn.sigmoid(gate_pre)
    hidden = (gate_pre * sigmoid_gate * up_pre).astype(jnp.bfloat16)
    partial_out = jnp.dot(hidden, down_slab, preferred_element_type=jnp.float32).astype(jnp.bfloat16)

    d_hidden = jnp.einsum("rd,fd->rf", grads_in, down_slab, preferred_element_type=jnp.float32)
    d_down = jnp.einsum("rf,rd->fd", hidden, grads_in, preferred_element_type=jnp.float32).astype(
        jnp.bfloat16
    )
    d_gate_act = (
        d_hidden * up_pre * sigmoid_gate * (1.0 + gate_pre * (1.0 - sigmoid_gate))
    ).astype(jnp.bfloat16)
    d_up_act = (d_hidden * gate_pre * sigmoid_gate).astype(jnp.bfloat16)
    d_gate = jnp.einsum(
        "rd,rf->df", gathered, d_gate_act, preferred_element_type=jnp.float32
    ).astype(jnp.bfloat16)
    d_up = jnp.einsum("rd,rf->df", gathered, d_up_act, preferred_element_type=jnp.float32).astype(
        jnp.bfloat16
    )

    blocks = partial_out.reshape(full.shape[0], capacity, d_all)
    on_chip = lax.psum_scatter(blocks, "core", scatter_dimension=0, tiled=True)
    summed_out = lax.psum_scatter(on_chip, "dpo", scatter_dimension=0, tiled=True)
    returned_out = lax.all_to_all(summed_out, "expert", split_axis=2, concat_axis=0, tiled=True)
    flat_out = returned_out.reshape(experts * capacity, -1).astype(jnp.float32)
    combined = jnp.dot(weighted.T, flat_out, precision=highest).astype(jnp.bfloat16)
    grads32 = out_grad.astype(jnp.float32)
    partial_dots = jnp.stack(
        [
            jnp.sum(grads32 * jnp.dot(picks[which].T, flat_out, precision=highest), axis=1)
            for which in range(top_count)
        ],
        axis=1,
    )
    d_route = lax.psum(partial_dots, "expert")
    return (combined, d_gate[None], d_up[None], d_down[None], d_route)


def solution(mesh):
    n_dp, n_exp = mesh.devices.shape
    split = Mesh(mesh.devices.reshape(n_dp // 2, 2, n_exp), ("dpo", "core", "expert"))
    return jax.shard_map(
        local,
        mesh=split,
        in_specs=(
            P(DP, "expert"),
            P(DP, "expert"),
            P(DP, None),
            P(DP, None),
            P("expert", None, DP),
            P("expert", None, DP),
            P("expert", DP, None),
        ),
        out_specs=(
            P(DP, "expert"),
            P("expert", None, DP),
            P("expert", None, DP),
            P("expert", DP, None),
            P(DP, None),
        ),
        check_vma=False,
    )
```

```python
import jax
import jax.numpy as jnp
from jax import lax
from jax.sharding import Mesh
from jax.sharding import PartitionSpec as P

highest = lax.Precision.HIGHEST
DP = ("dpo", "core")


def slot_table(routed, experts):
    flattened = routed.reshape(-1)
    onehot = (flattened[:, None] == jnp.arange(experts, dtype=jnp.int32)[None, :]).astype(jnp.int32)
    before = jnp.cumsum(onehot, axis=0) - onehot
    return jnp.sum(before * onehot, axis=1).reshape(routed.shape)


def pick_tables(routed, experts, capacity):
    places = slot_table(routed, experts)
    target = routed * capacity + places
    row_ids = jnp.arange(experts * capacity, dtype=jnp.int32)[:, None]
    return [
        (row_ids == target[None, :, which]).astype(jnp.float32) for which in range(routed.shape[1])
    ]


def local(tokens, out_grad, expert_ids, route_weights, w_gate, w_up, w_down):
    experts = lax.axis_size("expert")
    n_core = lax.axis_size("core")
    tok_rows, feat = tokens.shape
    top_count = expert_ids.shape[1]
    capacity = min(tok_rows, tok_rows * top_count * 33 // (32 * experts))
    picks = pick_tables(expert_ids, experts, capacity)
    dispatch = sum(picks)
    weighted = sum((picks[which] * route_weights[None, :, which] for which in range(top_count)))
    sent_tokens = jnp.dot(dispatch.astype(jnp.bfloat16), tokens, preferred_element_type=jnp.float32)
    sent_tokens = sent_tokens.astype(jnp.bfloat16).reshape(1, experts, capacity, feat)
    sent_grads = jnp.dot(weighted, out_grad.astype(jnp.float32), precision=highest)
    sent_grads = sent_grads.astype(jnp.bfloat16).reshape(1, experts, capacity, feat)
    sent = jnp.concatenate([sent_tokens, sent_grads], axis=0)
    recv = lax.all_to_all(sent, "expert", split_axis=1, concat_axis=3, tiled=True)

    def gather(part):
        half = lax.all_gather(part, "dpo", axis=0, tiled=True)
        return lax.all_gather(half, "core", axis=0, tiled=True)

    x_blocks = gather(recv[0])
    g_blocks = gather(recv[1])
    n_blk = x_blocks.shape[0]
    d_all = x_blocks.shape[2]
    n_rows = n_blk * capacity
    gathered = x_blocks.reshape(n_rows, d_all)
    grads_in = g_blocks.reshape(n_rows, d_all)
    gate_slab = w_gate[0]
    up_slab = w_up[0]
    down_slab = w_down[0]

    gate_pre = jnp.dot(gathered, gate_slab, preferred_element_type=jnp.float32)
    up_pre = jnp.dot(gathered, up_slab, preferred_element_type=jnp.float32)
    sigmoid_gate = jax.nn.sigmoid(gate_pre)
    hidden = (gate_pre * sigmoid_gate * up_pre).astype(jnp.bfloat16)
    partial_out = jnp.dot(hidden, down_slab, preferred_element_type=jnp.float32).astype(jnp.bfloat16)

    d_hidden = jnp.einsum("rd,fd->rf", grads_in, down_slab, preferred_element_type=jnp.float32)
    d_down = jnp.einsum("rf,rd->fd", hidden, grads_in, preferred_element_type=jnp.float32).astype(
        jnp.bfloat16
    )
    d_gate_act = (
        d_hidden * up_pre * sigmoid_gate * (1.0 + gate_pre * (1.0 - sigmoid_gate))
    ).astype(jnp.bfloat16)
    d_up_act = (d_hidden * gate_pre * sigmoid_gate).astype(jnp.bfloat16)
    d_gate = jnp.einsum(
        "rd,rf->df", gathered, d_gate_act, preferred_element_type=jnp.float32
    ).astype(jnp.bfloat16)
    d_up = jnp.einsum("rd,rf->df", gathered, d_up_act, preferred_element_type=jnp.float32).astype(
        jnp.bfloat16
    )

    blocks = partial_out.reshape(n_blk, capacity, experts, d_all // experts).transpose(0, 2, 1, 3)
    on_chip = lax.psum_scatter(blocks, "core", scatter_dimension=0, tiled=True)
    summed_out = lax.psum_scatter(on_chip, "dpo", scatter_dimension=0, tiled=True)
    returned_out = lax.all_to_all(summed_out, "expert", split_axis=1, concat_axis=0, tiled=True)
    flat_out = returned_out.reshape(experts * capacity, -1).astype(jnp.float32)
    combined = jnp.dot(weighted.T, flat_out, precision=highest).astype(jnp.bfloat16)
    grads32 = out_grad.astype(jnp.float32)
    partial_dots = jnp.stack(
        [
            jnp.sum(grads32 * jnp.dot(picks[which].T, flat_out, precision=highest), axis=1)
            for which in range(top_count)
        ],
        axis=1,
    )
    d_route = lax.psum(partial_dots, "expert")
    return (combined, d_gate[None], d_up[None], d_down[None], d_route)


def solution(mesh):
    n_dp, n_exp = mesh.devices.shape
    split = Mesh(mesh.devices.reshape(n_dp // 2, 2, n_exp), ("dpo", "core", "expert"))
    return jax.shard_map(
        local,
        mesh=split,
        in_specs=(
            P(DP, "expert"),
            P(DP, "expert"),
            P(DP, None),
            P(DP, None),
            P("expert", None, DP),
            P("expert", None, DP),
            P("expert", DP, None),
        ),
        out_specs=(
            P(DP, "expert"),
            P("expert", None, DP),
            P("expert", None, DP),
            P("expert", DP, None),
            P(DP, None),
        ),
        check_vma=False,
    )
```

```python
import jax
import jax.numpy as jnp
from jax import lax
from jax.sharding import Mesh
from jax.sharding import PartitionSpec as P

highest = lax.Precision.HIGHEST
DP = ("dpo", "core")


def slot_table(routed, experts):
    flattened = routed.reshape(-1)
    onehot = (flattened[:, None] == jnp.arange(experts, dtype=jnp.int32)[None, :]).astype(jnp.int32)
    before = jnp.cumsum(onehot, axis=0) - onehot
    return jnp.sum(before * onehot, axis=1).reshape(routed.shape)


def pick_tables(routed, experts, capacity):
    places = slot_table(routed, experts)
    target = routed * capacity + places
    row_ids = jnp.arange(experts * capacity, dtype=jnp.int32)[:, None]
    return [
        (row_ids == target[None, :, which]).astype(jnp.float32) for which in range(routed.shape[1])
    ]


def local(tokens, out_grad, expert_ids, route_weights, w_gate, w_up, w_down):
    experts = lax.axis_size("expert")
    n_core = lax.axis_size("core")
    tok_rows, feat = tokens.shape
    top_count = expert_ids.shape[1]
    capacity = min(tok_rows, tok_rows * top_count * 33 // (32 * experts))
    picks = pick_tables(expert_ids, experts, capacity)
    dispatch = sum(picks)
    weighted = sum((picks[which] * route_weights[None, :, which] for which in range(top_count)))
    sent_tokens = jnp.dot(dispatch.astype(jnp.bfloat16), tokens, preferred_element_type=jnp.float32)
    sent_tokens = sent_tokens.astype(jnp.bfloat16).reshape(1, experts, capacity, feat)
    sent_grads = jnp.dot(weighted, out_grad.astype(jnp.float32), precision=highest)
    sent_grads = sent_grads.astype(jnp.bfloat16).reshape(1, experts, capacity, feat)
    sent = jnp.concatenate([sent_tokens, sent_grads], axis=0)
    recv = lax.all_to_all(sent, "expert", split_axis=1, concat_axis=3, tiled=True)

    n_dp = lax.axis_size(DP)

    def gather(part):
        spread = jnp.broadcast_to(part, (n_dp,) + part.shape[1:])
        return lax.all_to_all(spread, DP, split_axis=0, concat_axis=0, tiled=True)

    x_blocks = gather(recv[0])
    g_blocks = gather(recv[1])
    n_blk = x_blocks.shape[0]
    d_all = x_blocks.shape[2]
    n_rows = n_blk * capacity
    gathered = x_blocks.reshape(n_rows, d_all)
    grads_in = g_blocks.reshape(n_rows, d_all)
    gate_slab = w_gate[0]
    up_slab = w_up[0]
    down_slab = w_down[0]

    gate_pre = jnp.dot(gathered, gate_slab, preferred_element_type=jnp.float32)
    up_pre = jnp.dot(gathered, up_slab, preferred_element_type=jnp.float32)
    sigmoid_gate = jax.nn.sigmoid(gate_pre)
    hidden = (gate_pre * sigmoid_gate * up_pre).astype(jnp.bfloat16)
    partial_out = jnp.dot(hidden, down_slab, preferred_element_type=jnp.float32).astype(jnp.bfloat16)

    d_hidden = jnp.einsum("rd,fd->rf", grads_in, down_slab, preferred_element_type=jnp.float32)
    d_down = jnp.einsum("rf,rd->fd", hidden, grads_in, preferred_element_type=jnp.float32).astype(
        jnp.bfloat16
    )
    d_gate_act = (
        d_hidden * up_pre * sigmoid_gate * (1.0 + gate_pre * (1.0 - sigmoid_gate))
    ).astype(jnp.bfloat16)
    d_up_act = (d_hidden * gate_pre * sigmoid_gate).astype(jnp.bfloat16)
    d_gate = jnp.einsum(
        "rd,rf->df", gathered, d_gate_act, preferred_element_type=jnp.float32
    ).astype(jnp.bfloat16)
    d_up = jnp.einsum("rd,rf->df", gathered, d_up_act, preferred_element_type=jnp.float32).astype(
        jnp.bfloat16
    )

    blocks = partial_out.reshape(n_blk, capacity, experts, d_all // experts).transpose(0, 2, 1, 3)
    slabs = lax.all_to_all(blocks, DP, split_axis=0, concat_axis=0, tiled=True)
    summed_out = jnp.sum(slabs.astype(jnp.float32), axis=0).astype(jnp.bfloat16)
    returned_out = lax.all_to_all(summed_out, "expert", split_axis=0, concat_axis=0, tiled=True)
    flat_out = returned_out.reshape(experts * capacity, -1).astype(jnp.float32)
    combined = jnp.dot(weighted.T, flat_out, precision=highest).astype(jnp.bfloat16)
    grads32 = out_grad.astype(jnp.float32)
    partial_dots = jnp.stack(
        [
            jnp.sum(grads32 * jnp.dot(picks[which].T, flat_out, precision=highest), axis=1)
            for which in range(top_count)
        ],
        axis=1,
    )
    d_route = lax.psum(partial_dots, "expert")
    return (combined, d_gate[None], d_up[None], d_down[None], d_route)


def solution(mesh):
    n_dp, n_exp = mesh.devices.shape
    split = Mesh(mesh.devices.reshape(n_dp // 2, 2, n_exp), ("dpo", "core", "expert"))
    return jax.shard_map(
        local,
        mesh=split,
        in_specs=(
            P(DP, "expert"),
            P(DP, "expert"),
            P(DP, None),
            P(DP, None),
            P("expert", None, DP),
            P("expert", None, DP),
            P("expert", DP, None),
        ),
        out_specs=(
            P(DP, "expert"),
            P("expert", None, DP),
            P("expert", None, DP),
            P("expert", DP, None),
            P(DP, None),
        ),
        check_vma=False,
    )
```

```python
import jax
import jax.numpy as jnp
from jax import lax
from jax.sharding import Mesh
from jax.sharding import PartitionSpec as P

highest = lax.Precision.HIGHEST
DP = ("dpo", "core")


def slot_table(routed, experts):
    flattened = routed.reshape(-1)
    onehot = (flattened[:, None] == jnp.arange(experts, dtype=jnp.int32)[None, :]).astype(jnp.int32)
    before = jnp.cumsum(onehot, axis=0) - onehot
    return jnp.sum(before * onehot, axis=1).reshape(routed.shape)


def pick_tables(routed, experts, capacity):
    places = slot_table(routed, experts)
    target = routed * capacity + places
    row_ids = jnp.arange(experts * capacity, dtype=jnp.int32)[:, None]
    return [
        (row_ids == target[None, :, which]).astype(jnp.float32) for which in range(routed.shape[1])
    ]


def local(tokens, out_grad, expert_ids, route_weights, w_gate, w_up, w_down):
    experts = lax.axis_size("expert")
    n_core = lax.axis_size("core")
    tok_rows, feat = tokens.shape
    top_count = expert_ids.shape[1]
    capacity = min(tok_rows, tok_rows * top_count * 33 // (32 * experts))
    picks = pick_tables(expert_ids, experts, capacity)
    dispatch = sum(picks)
    weighted = sum((picks[which] * route_weights[None, :, which] for which in range(top_count)))
    sent_tokens = jnp.dot(dispatch.astype(jnp.bfloat16), tokens, preferred_element_type=jnp.float32)
    sent_tokens = sent_tokens.astype(jnp.bfloat16).reshape(1, experts, capacity, feat)
    sent_grads = jnp.dot(weighted, out_grad.astype(jnp.float32), precision=highest)
    sent_grads = sent_grads.astype(jnp.bfloat16).reshape(1, experts, capacity, feat)
    sent = jnp.concatenate([sent_tokens, sent_grads], axis=0)
    recv = lax.all_to_all(sent, "expert", split_axis=1, concat_axis=3, tiled=True)

    both = jnp.concatenate([recv[0], recv[1]], axis=-1)
    blocks_all = lax.all_gather(both, DP, axis=0, tiled=True)
    n_blk = blocks_all.shape[0]
    d_all = recv.shape[-1]
    n_rows = n_blk * capacity
    gathered = blocks_all[:, :, :d_all].reshape(n_rows, d_all)
    grads_in = blocks_all[:, :, d_all:].reshape(n_rows, d_all)
    gate_slab = w_gate[0]
    up_slab = w_up[0]
    down_slab = w_down[0]

    gate_pre = jnp.dot(gathered, gate_slab, preferred_element_type=jnp.float32)
    up_pre = jnp.dot(gathered, up_slab, preferred_element_type=jnp.float32)
    sigmoid_gate = jax.nn.sigmoid(gate_pre)
    hidden = (gate_pre * sigmoid_gate * up_pre).astype(jnp.bfloat16)
    partial_out = jnp.dot(hidden, down_slab, preferred_element_type=jnp.float32).astype(jnp.bfloat16)

    d_hidden = jnp.einsum("rd,fd->rf", grads_in, down_slab, preferred_element_type=jnp.float32)
    d_down = jnp.einsum("rf,rd->fd", hidden, grads_in, preferred_element_type=jnp.float32).astype(
        jnp.bfloat16
    )
    d_gate_act = (
        d_hidden * up_pre * sigmoid_gate * (1.0 + gate_pre * (1.0 - sigmoid_gate))
    ).astype(jnp.bfloat16)
    d_up_act = (d_hidden * gate_pre * sigmoid_gate).astype(jnp.bfloat16)
    d_gate = jnp.einsum(
        "rd,rf->df", gathered, d_gate_act, preferred_element_type=jnp.float32
    ).astype(jnp.bfloat16)
    d_up = jnp.einsum("rd,rf->df", gathered, d_up_act, preferred_element_type=jnp.float32).astype(
        jnp.bfloat16
    )

    blocks = partial_out.reshape(n_blk, capacity, experts, d_all // experts).transpose(0, 2, 1, 3)
    summed_out = lax.psum_scatter(blocks, DP, scatter_dimension=0, tiled=True)
    returned_out = lax.all_to_all(summed_out, "expert", split_axis=1, concat_axis=0, tiled=True)
    flat_out = returned_out.reshape(experts * capacity, -1).astype(jnp.float32)
    combined = jnp.dot(weighted.T, flat_out, precision=highest).astype(jnp.bfloat16)
    grads32 = out_grad.astype(jnp.float32)
    partial_dots = jnp.stack(
        [
            jnp.sum(grads32 * jnp.dot(picks[which].T, flat_out, precision=highest), axis=1)
            for which in range(top_count)
        ],
        axis=1,
    )
    d_route = lax.psum(partial_dots, "expert")
    return (combined, d_gate[None], d_up[None], d_down[None], d_route)


def solution(mesh):
    n_dp, n_exp = mesh.devices.shape
    split = Mesh(mesh.devices.reshape(n_dp // 2, 2, n_exp), ("dpo", "core", "expert"))
    return jax.shard_map(
        local,
        mesh=split,
        in_specs=(
            P(DP, "expert"),
            P(DP, "expert"),
            P(DP, None),
            P(DP, None),
            P("expert", None, DP),
            P("expert", None, DP),
            P("expert", DP, None),
        ),
        out_specs=(
            P(DP, "expert"),
            P("expert", None, DP),
            P("expert", None, DP),
            P("expert", DP, None),
            P(DP, None),
        ),
        check_vma=False,
    )
```

```python
import jax
import jax.numpy as jnp
from jax import lax
from jax.sharding import Mesh
from jax.sharding import PartitionSpec as P

highest = lax.Precision.HIGHEST
DP = ("dpo", "core")


def slot_table(routed, experts):
    flattened = routed.reshape(-1)
    onehot = (flattened[:, None] == jnp.arange(experts, dtype=jnp.int32)[None, :]).astype(jnp.int32)
    before = jnp.cumsum(onehot, axis=0) - onehot
    return jnp.sum(before * onehot, axis=1).reshape(routed.shape)


def pick_tables(routed, experts, capacity):
    places = slot_table(routed, experts)
    target = routed * capacity + places
    row_ids = jnp.arange(experts * capacity, dtype=jnp.int32)[:, None]
    return [
        (row_ids == target[None, :, which]).astype(jnp.float32) for which in range(routed.shape[1])
    ]


def local(tokens, out_grad, expert_ids, route_weights, w_gate, w_up, w_down):
    experts = lax.axis_size("expert")
    n_core = lax.axis_size("core")
    tok_rows, feat = tokens.shape
    top_count = expert_ids.shape[1]
    capacity = min(tok_rows, tok_rows * top_count * 33 // (32 * experts))
    picks = pick_tables(expert_ids, experts, capacity)
    dispatch = sum(picks)
    weighted = sum((picks[which] * route_weights[None, :, which] for which in range(top_count)))
    sent_tokens = jnp.dot(dispatch.astype(jnp.bfloat16), tokens, preferred_element_type=jnp.float32)
    sent_tokens = sent_tokens.astype(jnp.bfloat16).reshape(1, experts, capacity, feat)
    sent_grads = jnp.dot(weighted, out_grad.astype(jnp.float32), precision=highest)
    sent_grads = sent_grads.astype(jnp.bfloat16).reshape(1, experts, capacity, feat)
    sent = jnp.concatenate([sent_tokens, sent_grads], axis=0)
    recv = lax.all_to_all(sent, "expert", split_axis=1, concat_axis=3, tiled=True)

    both = jnp.concatenate([recv[0], recv[1]], axis=-1)
    blocks_all = lax.all_gather(both, DP, axis=0, tiled=True)
    n_blk = blocks_all.shape[0]
    d_all = recv.shape[-1]
    n_rows = n_blk * capacity
    flat_all = blocks_all.reshape(n_rows, 2 * d_all)
    gathered = flat_all[:, :d_all]
    grads_in = flat_all[:, d_all:]
    gate_slab = w_gate[0]
    up_slab = w_up[0]
    down_slab = w_down[0]

    gate_pre = jnp.dot(gathered, gate_slab, preferred_element_type=jnp.float32)
    up_pre = jnp.dot(gathered, up_slab, preferred_element_type=jnp.float32)
    sigmoid_gate = jax.nn.sigmoid(gate_pre)
    hidden = (gate_pre * sigmoid_gate * up_pre).astype(jnp.bfloat16)
    partial_out = jnp.dot(hidden, down_slab, preferred_element_type=jnp.float32).astype(jnp.bfloat16)

    d_hidden = jnp.einsum("rd,fd->rf", grads_in, down_slab, preferred_element_type=jnp.float32)
    d_down = jnp.einsum("rf,rd->fd", hidden, grads_in, preferred_element_type=jnp.float32).astype(
        jnp.bfloat16
    )
    d_gate_act = (
        d_hidden * up_pre * sigmoid_gate * (1.0 + gate_pre * (1.0 - sigmoid_gate))
    ).astype(jnp.bfloat16)
    d_up_act = (d_hidden * gate_pre * sigmoid_gate).astype(jnp.bfloat16)
    d_gate = jnp.einsum(
        "rd,rf->df", gathered, d_gate_act, preferred_element_type=jnp.float32
    ).astype(jnp.bfloat16)
    d_up = jnp.einsum("rd,rf->df", gathered, d_up_act, preferred_element_type=jnp.float32).astype(
        jnp.bfloat16
    )

    blocks = partial_out.reshape(n_blk, capacity, experts, d_all // experts).transpose(0, 2, 1, 3)
    summed_out = lax.psum_scatter(blocks, DP, scatter_dimension=0, tiled=True)
    returned_out = lax.all_to_all(summed_out, "expert", split_axis=1, concat_axis=0, tiled=True)
    flat_out = returned_out.reshape(experts * capacity, -1).astype(jnp.float32)
    combined = jnp.dot(weighted.T, flat_out, precision=highest).astype(jnp.bfloat16)
    grads32 = out_grad.astype(jnp.float32)
    partial_dots = jnp.stack(
        [
            jnp.sum(grads32 * jnp.dot(picks[which].T, flat_out, precision=highest), axis=1)
            for which in range(top_count)
        ],
        axis=1,
    )
    d_route = lax.psum(partial_dots, "expert")
    return (combined, d_gate[None], d_up[None], d_down[None], d_route)


def solution(mesh):
    n_dp, n_exp = mesh.devices.shape
    split = Mesh(mesh.devices.reshape(n_dp // 2, 2, n_exp), ("dpo", "core", "expert"))
    return jax.shard_map(
        local,
        mesh=split,
        in_specs=(
            P(DP, "expert"),
            P(DP, "expert"),
            P(DP, None),
            P(DP, None),
            P("expert", None, DP),
            P("expert", None, DP),
            P("expert", DP, None),
        ),
        out_specs=(
            P(DP, "expert"),
            P("expert", None, DP),
            P("expert", None, DP),
            P("expert", DP, None),
            P(DP, None),
        ),
        check_vma=False,
    )
```

```python
import jax
import jax.numpy as jnp
from jax import lax
from jax.sharding import Mesh
from jax.sharding import PartitionSpec as P

highest = lax.Precision.HIGHEST
DP = ("dpo", "core")


def slot_table(routed, experts):
    flattened = routed.reshape(-1)
    onehot = (flattened[:, None] == jnp.arange(experts, dtype=jnp.int32)[None, :]).astype(jnp.int32)
    before = jnp.cumsum(onehot, axis=0) - onehot
    return jnp.sum(before * onehot, axis=1).reshape(routed.shape)


def pick_tables(routed, experts, capacity):
    places = slot_table(routed, experts)
    target = routed * capacity + places
    row_ids = jnp.arange(experts * capacity, dtype=jnp.int32)[:, None]
    return [
        (row_ids == target[None, :, which]).astype(jnp.float32) for which in range(routed.shape[1])
    ]


def local(tokens, out_grad, expert_ids, route_weights, w_gate, w_up, w_down):
    experts = lax.axis_size("expert")
    n_core = lax.axis_size("core")
    tok_rows, feat = tokens.shape
    top_count = expert_ids.shape[1]
    capacity = min(tok_rows, tok_rows * top_count * 33 // (32 * experts))
    picks = pick_tables(expert_ids, experts, capacity)
    dispatch = sum(picks)
    weighted = sum((picks[which] * route_weights[None, :, which] for which in range(top_count)))
    sent_tokens = jnp.dot(dispatch.astype(jnp.bfloat16), tokens, preferred_element_type=jnp.float32)
    sent_tokens = sent_tokens.astype(jnp.bfloat16).reshape(1, experts, capacity, feat)
    sent_grads = jnp.dot(weighted, out_grad.astype(jnp.float32), precision=highest)
    sent_grads = sent_grads.astype(jnp.bfloat16).reshape(1, experts, capacity, feat)
    sent_raw = jnp.dot(dispatch.astype(jnp.bfloat16), out_grad, preferred_element_type=jnp.float32)
    sent_raw = sent_raw.astype(jnp.bfloat16).reshape(1, experts, capacity, feat)
    sent = jnp.concatenate([sent_tokens, sent_grads, sent_raw], axis=0)
    recv = lax.all_to_all(sent, "expert", split_axis=1, concat_axis=3, tiled=True)

    both = jnp.concatenate([recv[0], recv[1]], axis=-1)
    blocks_all = lax.all_gather(both, DP, axis=0, tiled=True)
    n_blk = blocks_all.shape[0]
    d_all = recv.shape[-1]
    n_rows = n_blk * capacity
    flat_all = blocks_all.reshape(n_rows, 2 * d_all)
    gathered = flat_all[:, :d_all]
    grads_in = flat_all[:, d_all:]
    gate_slab = w_gate[0]
    up_slab = w_up[0]
    down_slab = w_down[0]

    gate_pre = jnp.dot(gathered, gate_slab, preferred_element_type=jnp.float32)
    up_pre = jnp.dot(gathered, up_slab, preferred_element_type=jnp.float32)
    sigmoid_gate = jax.nn.sigmoid(gate_pre)
    hidden = (gate_pre * sigmoid_gate * up_pre).astype(jnp.bfloat16)
    partial_out = jnp.dot(hidden, down_slab, preferred_element_type=jnp.float32).astype(jnp.bfloat16)

    d_hidden = jnp.einsum("rd,fd->rf", grads_in, down_slab, preferred_element_type=jnp.float32)
    d_down = jnp.einsum("rf,rd->fd", hidden, grads_in, preferred_element_type=jnp.float32).astype(
        jnp.bfloat16
    )
    d_gate_act = (
        d_hidden * up_pre * sigmoid_gate * (1.0 + gate_pre * (1.0 - sigmoid_gate))
    ).astype(jnp.bfloat16)
    d_up_act = (d_hidden * gate_pre * sigmoid_gate).astype(jnp.bfloat16)
    d_gate = jnp.einsum(
        "rd,rf->df", gathered, d_gate_act, preferred_element_type=jnp.float32
    ).astype(jnp.bfloat16)
    d_up = jnp.einsum("rd,rf->df", gathered, d_up_act, preferred_element_type=jnp.float32).astype(
        jnp.bfloat16
    )

    blocks = partial_out.reshape(n_blk, capacity, experts, d_all // experts).transpose(0, 2, 1, 3)
    summed_out = lax.psum_scatter(blocks, DP, scatter_dimension=0, tiled=True)
    raw_rows = recv[2, 0].reshape(capacity, experts, d_all // experts).astype(jnp.float32)
    dots = jnp.einsum("cfj,fcj->c", raw_rows, summed_out[0].astype(jnp.float32), precision=highest)
    hi = lax.reduce_precision(dots, exponent_bits=8, mantissa_bits=7)
    rest = dots - hi
    mid = lax.reduce_precision(rest, exponent_bits=8, mantissa_bits=7)
    lo = rest - mid
    pieces = jnp.stack([hi, mid, lo], axis=1).astype(jnp.bfloat16)
    lanes = jnp.pad(pieces, ((0, 0), (0, 128 - pieces.shape[1])))
    lanes = jnp.broadcast_to(lanes[None, None], (1, experts) + lanes.shape)
    payload = jnp.concatenate([summed_out, lanes], axis=-1)
    returned = lax.all_to_all(payload, "expert", split_axis=1, concat_axis=0, tiled=True)
    returned_out = returned[..., : d_all // experts]
    got = returned[..., d_all // experts : d_all // experts + 3].astype(jnp.float32)
    dots_all = ((got[..., 0] + got[..., 1]) + got[..., 2]).reshape(-1)
    flat_out = returned_out.reshape(experts * capacity, -1).astype(jnp.float32)
    combined = jnp.dot(weighted.T, flat_out, precision=highest).astype(jnp.bfloat16)
    target = expert_ids * capacity + slot_table(expert_ids, experts)
    d_route = dots_all[target]
    return (combined, d_gate[None], d_up[None], d_down[None], d_route)


def solution(mesh):
    n_dp, n_exp = mesh.devices.shape
    split = Mesh(mesh.devices.reshape(n_dp // 2, 2, n_exp), ("dpo", "core", "expert"))
    return jax.shard_map(
        local,
        mesh=split,
        in_specs=(
            P(DP, "expert"),
            P(DP, "expert"),
            P(DP, None),
            P(DP, None),
            P("expert", None, DP),
            P("expert", None, DP),
            P("expert", DP, None),
        ),
        out_specs=(
            P(DP, "expert"),
            P("expert", None, DP),
            P("expert", None, DP),
            P("expert", DP, None),
            P(DP, None),
        ),
        check_vma=False,
    )
```

```python
import jax
import jax.numpy as jnp
from jax import lax
from jax.sharding import Mesh
from jax.sharding import PartitionSpec as P

highest = lax.Precision.HIGHEST
DP = ("dpo", "core")


def slot_table(routed, experts):
    flattened = routed.reshape(-1)
    onehot = (flattened[:, None] == jnp.arange(experts, dtype=jnp.int32)[None, :]).astype(jnp.int32)
    before = jnp.cumsum(onehot, axis=0) - onehot
    return jnp.sum(before * onehot, axis=1).reshape(routed.shape)


def pick_tables(routed, experts, capacity):
    places = slot_table(routed, experts)
    target = routed * capacity + places
    row_ids = jnp.arange(experts * capacity, dtype=jnp.int32)[:, None]
    return [
        (row_ids == target[None, :, which]).astype(jnp.float32) for which in range(routed.shape[1])
    ]


def local(tokens, out_grad, expert_ids, route_weights, w_gate, w_up, w_down):
    experts = lax.axis_size("expert")
    n_core = lax.axis_size("core")
    tok_rows, feat = tokens.shape
    top_count = expert_ids.shape[1]
    capacity = min(tok_rows, tok_rows * top_count * 33 // (32 * experts))
    picks = pick_tables(expert_ids, experts, capacity)
    dispatch = sum(picks)
    weighted = sum((picks[which] * route_weights[None, :, which] for which in range(top_count)))
    sent_tokens = jnp.dot(dispatch.astype(jnp.bfloat16), tokens, preferred_element_type=jnp.float32)
    sent_tokens = sent_tokens.astype(jnp.bfloat16).reshape(1, experts, capacity, feat)
    sent_grads = jnp.dot(weighted, out_grad.astype(jnp.float32), precision=highest)
    sent_grads = sent_grads.astype(jnp.bfloat16).reshape(1, experts, capacity, feat)
    sent_raw = jnp.dot(dispatch.astype(jnp.bfloat16), out_grad, preferred_element_type=jnp.float32)
    sent_raw = sent_raw.astype(jnp.bfloat16).reshape(1, experts, capacity, feat)
    sent = jnp.concatenate([sent_tokens, sent_grads, sent_raw], axis=0)
    recv = lax.all_to_all(sent, "expert", split_axis=1, concat_axis=3, tiled=True)

    both = jnp.concatenate([recv[0], recv[1]], axis=-1)
    blocks_all = lax.all_gather(both, DP, axis=0, tiled=True)
    n_blk = blocks_all.shape[0]
    d_all = recv.shape[-1]
    n_rows = n_blk * capacity
    flat_all = blocks_all.reshape(n_rows, 2 * d_all)
    gathered = flat_all[:, :d_all]
    grads_in = flat_all[:, d_all:]
    gate_slab = w_gate[0]
    up_slab = w_up[0]
    down_slab = w_down[0]

    gate_pre = jnp.dot(gathered, gate_slab, preferred_element_type=jnp.float32)
    up_pre = jnp.dot(gathered, up_slab, preferred_element_type=jnp.float32)
    sigmoid_gate = jax.nn.sigmoid(gate_pre)
    hidden = (gate_pre * sigmoid_gate * up_pre).astype(jnp.bfloat16)
    partial_out = jnp.dot(hidden, down_slab, preferred_element_type=jnp.float32).astype(jnp.bfloat16)

    d_hidden = jnp.einsum("rd,fd->rf", grads_in, down_slab, preferred_element_type=jnp.float32)
    d_down = jnp.einsum("rf,rd->fd", hidden, grads_in, preferred_element_type=jnp.float32).astype(
        jnp.bfloat16
    )
    d_gate_act = (
        d_hidden * up_pre * sigmoid_gate * (1.0 + gate_pre * (1.0 - sigmoid_gate))
    ).astype(jnp.bfloat16)
    d_up_act = (d_hidden * gate_pre * sigmoid_gate).astype(jnp.bfloat16)
    d_gate = jnp.einsum(
        "rd,rf->df", gathered, d_gate_act, preferred_element_type=jnp.float32
    ).astype(jnp.bfloat16)
    d_up = jnp.einsum("rd,rf->df", gathered, d_up_act, preferred_element_type=jnp.float32).astype(
        jnp.bfloat16
    )

    blocks = partial_out.reshape(n_blk, capacity, experts, d_all // experts).transpose(0, 2, 1, 3)
    dj = d_all // experts
    blocks = blocks.reshape(n_blk // n_core, n_core, experts, capacity, dj).transpose(1, 0, 2, 3, 4)
    blocks = blocks.reshape(n_blk, experts, capacity, dj)
    on_chip = lax.psum_scatter(blocks, "core", scatter_dimension=0, tiled=True)
    summed_out = lax.psum_scatter(on_chip, "dpo", scatter_dimension=0, tiled=True)
    raw_rows = recv[2, 0].reshape(capacity, experts, d_all // experts).astype(jnp.float32)
    dots = jnp.einsum("cfj,fcj->c", raw_rows, summed_out[0].astype(jnp.float32), precision=highest)
    hi = lax.reduce_precision(dots, exponent_bits=8, mantissa_bits=7)
    rest = dots - hi
    mid = lax.reduce_precision(rest, exponent_bits=8, mantissa_bits=7)
    lo = rest - mid
    pieces = jnp.stack([hi, mid, lo], axis=1).astype(jnp.bfloat16)
    lanes = jnp.pad(pieces, ((0, 0), (0, 128 - pieces.shape[1])))
    lanes = jnp.broadcast_to(lanes[None, None], (1, experts) + lanes.shape)
    payload = jnp.concatenate([summed_out, lanes], axis=-1)
    returned = lax.all_to_all(payload, "expert", split_axis=1, concat_axis=0, tiled=True)
    returned_out = returned[..., : d_all // experts]
    got = returned[..., d_all // experts : d_all // experts + 3].astype(jnp.float32)
    dots_all = ((got[..., 0] + got[..., 1]) + got[..., 2]).reshape(-1)
    flat_out = returned_out.reshape(experts * capacity, -1).astype(jnp.float32)
    combined = jnp.dot(weighted.T, flat_out, precision=highest).astype(jnp.bfloat16)
    target = expert_ids * capacity + slot_table(expert_ids, experts)
    d_route = dots_all[target]
    return (combined, d_gate[None], d_up[None], d_down[None], d_route)


def solution(mesh):
    n_dp, n_exp = mesh.devices.shape
    split = Mesh(mesh.devices.reshape(n_dp // 2, 2, n_exp), ("dpo", "core", "expert"))
    return jax.shard_map(
        local,
        mesh=split,
        in_specs=(
            P(DP, "expert"),
            P(DP, "expert"),
            P(DP, None),
            P(DP, None),
            P("expert", None, DP),
            P("expert", None, DP),
            P("expert", DP, None),
        ),
        out_specs=(
            P(DP, "expert"),
            P("expert", None, DP),
            P("expert", None, DP),
            P("expert", DP, None),
            P(DP, None),
        ),
        check_vma=False,
    )
```

```python
import jax
import jax.numpy as jnp
from jax import lax
from jax.sharding import Mesh
from jax.sharding import PartitionSpec as P

highest = lax.Precision.HIGHEST
DP = ("dpo", "core")


def slot_table(routed, experts):
    flattened = routed.reshape(-1)
    onehot = (flattened[:, None] == jnp.arange(experts, dtype=jnp.int32)[None, :]).astype(jnp.int32)
    before = jnp.cumsum(onehot, axis=0) - onehot
    return jnp.sum(before * onehot, axis=1).reshape(routed.shape)


def pick_tables(routed, experts, capacity):
    places = slot_table(routed, experts)
    target = routed * capacity + places
    row_ids = jnp.arange(experts * capacity, dtype=jnp.int32)[:, None]
    return [
        (row_ids == target[None, :, which]).astype(jnp.float32) for which in range(routed.shape[1])
    ]


def local(tokens, out_grad, expert_ids, route_weights, w_gate, w_up, w_down):
    experts = lax.axis_size("expert")
    n_core = lax.axis_size("core")
    tok_rows, feat = tokens.shape
    top_count = expert_ids.shape[1]
    capacity = min(tok_rows, tok_rows * top_count * 33 // (32 * experts))
    picks = pick_tables(expert_ids, experts, capacity)
    dispatch = sum(picks)
    weighted = sum((picks[which] * route_weights[None, :, which] for which in range(top_count)))
    sent_tokens = jnp.dot(dispatch.astype(jnp.bfloat16), tokens, preferred_element_type=jnp.float32)
    sent_tokens = sent_tokens.astype(jnp.bfloat16).reshape(1, experts, capacity, feat)
    sent_grads = jnp.dot(weighted, out_grad.astype(jnp.float32), precision=highest)
    sent_grads = sent_grads.astype(jnp.bfloat16).reshape(1, experts, capacity, feat)
    sent_raw = jnp.dot(dispatch.astype(jnp.bfloat16), out_grad, preferred_element_type=jnp.float32)
    sent_raw = sent_raw.astype(jnp.bfloat16).reshape(1, experts, capacity, feat)
    sent = jnp.concatenate([sent_tokens, sent_grads, sent_raw], axis=0)
    recv = lax.all_to_all(sent, "expert", split_axis=1, concat_axis=3, tiled=True)

    both = jnp.concatenate([recv[0], recv[1]], axis=-1)
    blocks_all = lax.all_gather(both, DP, axis=0, tiled=True)
    n_blk = blocks_all.shape[0]
    d_all = recv.shape[-1]
    n_rows = n_blk * capacity
    gathered = blocks_all[:, :, :d_all]
    grads_in = blocks_all[:, :, d_all:]
    gate_slab = w_gate[0]
    up_slab = w_up[0]
    down_slab = w_down[0]

    gate_pre = jnp.einsum("gcd,df->gcf", gathered, gate_slab, preferred_element_type=jnp.float32)
    up_pre = jnp.einsum("gcd,df->gcf", gathered, up_slab, preferred_element_type=jnp.float32)
    sigmoid_gate = jax.nn.sigmoid(gate_pre)
    hidden = (gate_pre * sigmoid_gate * up_pre).astype(jnp.bfloat16)
    partial_out = jnp.einsum("gcf,fd->gcd", hidden, down_slab, preferred_element_type=jnp.float32).astype(jnp.bfloat16)

    d_hidden = jnp.einsum("gcd,fd->gcf", grads_in, down_slab, preferred_element_type=jnp.float32)
    d_down = jnp.einsum("gcf,gcd->fd", hidden, grads_in, preferred_element_type=jnp.float32).astype(
        jnp.bfloat16
    )
    d_gate_act = (
        d_hidden * up_pre * sigmoid_gate * (1.0 + gate_pre * (1.0 - sigmoid_gate))
    ).astype(jnp.bfloat16)
    d_up_act = (d_hidden * gate_pre * sigmoid_gate).astype(jnp.bfloat16)
    d_gate = jnp.einsum(
        "gcd,gcf->df", gathered, d_gate_act, preferred_element_type=jnp.float32
    ).astype(jnp.bfloat16)
    d_up = jnp.einsum("gcd,gcf->df", gathered, d_up_act, preferred_element_type=jnp.float32).astype(
        jnp.bfloat16
    )

    blocks = partial_out.reshape(n_blk, capacity, experts, d_all // experts).transpose(0, 2, 1, 3)
    summed_out = lax.psum_scatter(blocks, DP, scatter_dimension=0, tiled=True)
    raw_rows = recv[2, 0].reshape(capacity, experts, d_all // experts).astype(jnp.float32)
    dots = jnp.einsum("cfj,fcj->c", raw_rows, summed_out[0].astype(jnp.float32), precision=highest)
    hi = lax.reduce_precision(dots, exponent_bits=8, mantissa_bits=7)
    rest = dots - hi
    mid = lax.reduce_precision(rest, exponent_bits=8, mantissa_bits=7)
    lo = rest - mid
    pieces = jnp.stack([hi, mid, lo], axis=1).astype(jnp.bfloat16)
    lanes = jnp.pad(pieces, ((0, 0), (0, 128 - pieces.shape[1])))
    lanes = jnp.broadcast_to(lanes[None, None], (1, experts) + lanes.shape)
    payload = jnp.concatenate([summed_out, lanes], axis=-1)
    returned = lax.all_to_all(payload, "expert", split_axis=1, concat_axis=0, tiled=True)
    returned_out = returned[..., : d_all // experts]
    got = returned[..., d_all // experts : d_all // experts + 3].astype(jnp.float32)
    dots_all = ((got[..., 0] + got[..., 1]) + got[..., 2]).reshape(-1)
    flat_out = returned_out.reshape(experts * capacity, -1).astype(jnp.float32)
    combined = jnp.dot(weighted.T, flat_out, precision=highest).astype(jnp.bfloat16)
    target = expert_ids * capacity + slot_table(expert_ids, experts)
    d_route = dots_all[target]
    return (combined, d_gate[None], d_up[None], d_down[None], d_route)


def solution(mesh):
    n_dp, n_exp = mesh.devices.shape
    split = Mesh(mesh.devices.reshape(n_dp // 2, 2, n_exp), ("dpo", "core", "expert"))
    return jax.shard_map(
        local,
        mesh=split,
        in_specs=(
            P(DP, "expert"),
            P(DP, "expert"),
            P(DP, None),
            P(DP, None),
            P("expert", None, DP),
            P("expert", None, DP),
            P("expert", DP, None),
        ),
        out_specs=(
            P(DP, "expert"),
            P("expert", None, DP),
            P("expert", None, DP),
            P("expert", DP, None),
            P(DP, None),
        ),
        check_vma=False,
    )
```
